32 devices in a mesh: dp: 8 (over z, x), expert: 4 (over y, core).
Axes of the slice: x: 2, y: 2, z: 4, core: 2. Of those that a mesh axis runs over, the one named last changes fastest.
Arguments:
- tokens: bfloat16 [4096, 1024], P(('dp', 'expert')), may hold values from -6 to 6
- expert_ids: int32 [4096, 8], P(('dp', 'expert')), may hold values from 0 to 15, as said below
- slot_index: int32 [4096, 8], P(('dp', 'expert')), may hold values from -1 to 63, as said below
- combine_weight: bfloat16 [4096, 8], P(('dp', 'expert')), may hold values from 0.099609375 to 0.8984375
- talker_owner: int32 [4096], P(('dp', 'expert')), may hold values from 0 to 7, as said below
- gate_weight: bfloat16 [16, 1024, 384], P('expert'), may hold values from -0.1875 to 0.1875
- up_weight: bfloat16 [16, 1024, 384], P('expert'), may hold values from -0.1875 to 0.1875
- down_weight: bfloat16 [16, 1024, 384], P('expert'), may hold values from -0.3125 to 0.3125
- grad_talker: bfloat16 [4096, 1024], P(('dp', 'expert')), may hold values from -3 to 3
Outputs:
- talker_out: bfloat16 [4096, 1024], P(('dp', 'expert'))
- grad_tokens: bfloat16 [4096, 1024], P(('dp', 'expert'))
- grad_gate: float32 [16, 1024, 384], P('expert', 'dp')
- grad_up: float32 [16, 1024, 384], P('expert', 'dp')
- grad_down: float32 [16, 1024, 384], P('expert', 'dp')
The draws below stay inside these ranges and needn't reach their ends.
Inputs may be any that keep to these rules, and one draw needn't show every extreme that they name: `expert_ids`: each row names 8 different experts; one expert is named by every row. `slot_index`: for the pairs of one device's 128 rows that name one expert, taken in row order, the slot is the pair's rank among them when under 64, else -1; on every device some expert fills all 64 slots. `talker_owner`: among one device's 128 rows each owner appears exactly 16 times.
All inputs are finite; a program needn't handle non-finite values.
Results may differ from the reference program's by a relative error of at most 0.02.
Values may be sent and summed in bfloat16 or wider, within the bound.
A program may use at most 64 MiB of HBM per device.

```python
import jax
import jax.numpy as jnp
from jax import lax

D = 1024
FF = 384
EXPERTS = 16
TOPK = 8
TOK_DEV = 128
CAP = 64
DATA_DEVS = 8
PER_OWNER = 16
TOKENS = 4096
N_DP = 8
N_EXPERT = 4


def routing_draw(key):
    base = jax.random.fold_in(key, 7)
    key_hot, key_bias, key_noise = jax.random.split(base, 3)
    hottest = jax.random.randint(key_hot, (), 0, EXPERTS)
    leaning = jax.random.randint(key_bias, (EXPERTS,), 0, 2048)
    noise = jax.random.randint(key_noise, (TOKENS, EXPERTS), 0, 4096)
    column = jnp.arange(EXPERTS, dtype=jnp.int32)
    score = noise + leaning[None, :] + jnp.where(column == hottest, 1 << 20, 0)[None, :]
    score = score * EXPERTS + column[None, :]
    picked = lax.top_k(score, TOPK)[1].astype(jnp.int32)
    blocks = TOKENS // TOK_DEV
    chosen = picked.reshape(blocks, TOK_DEV, TOPK)
    onehot = jnp.sum((chosen[..., None] == column).astype(jnp.int32), axis=2, dtype=jnp.int32)
    before = jnp.cumsum(onehot, axis=1, dtype=jnp.int32) - onehot
    ranked = jnp.take_along_axis(before, chosen, axis=2)
    slot_ids = jnp.where(ranked < CAP, ranked, -1).astype(jnp.int32)
    return (picked, slot_ids.reshape(TOKENS, TOPK))


def draw_expert_ids(key, part):
    return routing_draw(key)[0]


def draw_slot_index(key, part):
    return routing_draw(key)[1]


def draw_talker_owner(key, part):
    base = jax.random.fold_in(key, 13)
    blocks = TOKENS // TOK_DEV
    score = jax.random.randint(base, (blocks, TOK_DEV), 0, 1 << 16) * TOK_DEV + jnp.arange(TOK_DEV, dtype=jnp.int32)[None, :]
    order = jnp.argsort(score, axis=1, stable=True).astype(jnp.int32)
    return (order % DATA_DEVS).reshape(TOKENS).astype(jnp.int32)


def steps_of(key, dims, shards, low, high):
    loudness, own = 1.0, jax.random.fold_in(key, 6)
    for dim, shards_of in shards:
        steps = jnp.exp(jax.random.uniform(jax.random.fold_in(own, dim), (shards_of,), jnp.float32, low / len(shards), high / len(shards)))
        loudness = loudness * jnp.repeat(steps, dims[dim] // shards_of).reshape([-1 if axis == dim else 1 for axis in range(len(dims))])
    return loudness


def centred(own_key, extent, spread, most, pieces=(), held_as=jnp.bfloat16):
    factor_of = steps_of(own_key, extent, pieces, -0.22, 0.18) if pieces else 1.0
    drawn = jax.random.normal(own_key, extent, jnp.float32) * spread * factor_of
    return jnp.minimum(jnp.maximum(drawn, -most), most).astype(held_as)


def setup_inputs(seed: int = 0) -> dict:
    key_list = jax.random.split(jax.random.key(seed), 10)
    return {
        "tokens": centred(key_list[0], (TOKENS, D), 1.0, 6.0, ((0, 32),)),
        "expert_ids": draw_expert_ids(jax.random.fold_in(key_list[9], 71), 0),
        "slot_index": draw_slot_index(jax.random.fold_in(key_list[9], 71), 0),
        "combine_weight": jnp.clip(0.099609375 + 0.7988281 * jax.random.uniform(key_list[3], (TOKENS, TOPK), jnp.float32) ** steps_of(key_list[3], (TOKENS, TOPK), ((0, 32),), -0.2, 0.2), 0.099609375, 0.8984375).astype(jnp.bfloat16),
        "talker_owner": draw_talker_owner(jax.random.fold_in(key_list[9], 71), 0),
        "gate_weight": centred(key_list[5], (EXPERTS, D, FF), D ** -0.5, 0.1875, ((0, 4),)),
        "up_weight": centred(key_list[6], (EXPERTS, D, FF), D ** -0.5, 0.1875, ((0, 4),)),
        "down_weight": centred(key_list[7], (EXPERTS, D, FF), FF ** -0.5, 0.3125, ((0, 4),)),
        "grad_talker": centred(key_list[8], (TOKENS, D), 0.5, 3.0, ((0, 32),)),
    }


def pad_row(values, axis):
    extra_shape = list(values.shape)
    extra_shape[axis] = 1
    return jnp.concatenate([values, jnp.zeros(tuple(extra_shape), values.dtype)], axis)


def slot_table(route_ids, route_slots):
    row_count, pair_width = route_ids.shape
    slot_count = EXPERTS * CAP
    position = jnp.where(route_slots >= 0, route_ids * CAP + route_slots, slot_count).astype(jnp.int32)
    pair_table = jnp.full((slot_count + 1,), row_count * pair_width, jnp.int32)
    pair_table = pair_table.at[position.reshape(-1)].set(jnp.arange(row_count * pair_width, dtype=jnp.int32))
    return pair_table[:slot_count], position


def owner_position(owner_ids):
    onehot = (owner_ids[:, None] == jnp.arange(DATA_DEVS, dtype=jnp.int32)[None, :]).astype(jnp.int32)
    before = jnp.cumsum(onehot, axis=0, dtype=jnp.int32) - onehot
    ranked = jnp.sum(before * onehot, axis=1, dtype=jnp.int32)
    return (owner_ids * PER_OWNER + ranked).astype(jnp.int32)


def invert_slots(slot_ids):
    return jnp.zeros((TOK_DEV,), jnp.int32).at[slot_ids].set(jnp.arange(TOK_DEV, dtype=jnp.int32))


def accumulate(total, part):
    return total + lax.optimization_barrier(part.astype(jnp.bfloat16)).astype(jnp.float32)


def reference(tokens, expert_ids, slot_index, combine_weight, talker_owner, gate_weight, up_weight, down_weight, grad_talker):
    data_devs = N_DP
    expert_devs = N_EXPERT
    token_blocks = tokens.reshape(data_devs, expert_devs, TOK_DEV, D)
    id_blocks = expert_ids.reshape(data_devs, expert_devs, TOK_DEV, TOPK)
    slot_blocks = slot_index.reshape(data_devs, expert_devs, TOK_DEV, TOPK)
    weight_blocks = combine_weight.reshape(data_devs, expert_devs, TOK_DEV, TOPK)
    owner_blocks = talker_owner.reshape(data_devs, expert_devs, TOK_DEV)
    owner_slot = jax.vmap(jax.vmap(owner_position))(owner_blocks)
    arranged = grad_talker.reshape(data_devs, expert_devs, data_devs, PER_OWNER, D)
    arranged = arranged.transpose(2, 1, 0, 3, 4).reshape(data_devs, expert_devs, TOK_DEV, D)
    upstream = jnp.take_along_axis(arranged, owner_slot[..., None], axis=2)
    gate32 = gate_weight.astype(jnp.float32)
    up32 = up_weight.astype(jnp.float32)
    down32 = down_weight.astype(jnp.float32)

    def group(totals, blocks_in):
        block_tokens, block_ids, block_slots, block_weights, block_upstream = blocks_in
        pair_tables, positions = jax.vmap(slot_table)(block_ids, block_slots)
        row_tables = pair_tables // TOPK
        flat_positions = positions.reshape(expert_devs, TOK_DEV * TOPK)[..., None]
        dispatched = jnp.take_along_axis(pad_row(block_tokens, 1), row_tables[..., None], axis=1)
        dispatched = dispatched.reshape(expert_devs, EXPERTS, CAP, D).transpose(1, 0, 2, 3)
        inputs32 = dispatched.astype(jnp.float32)
        gate_pre = jnp.einsum("escd,edf->escf", inputs32, gate32)
        up_pre = jnp.einsum("escd,edf->escf", inputs32, up32)
        hidden = (jax.nn.silu(gate_pre) * up_pre).astype(jnp.bfloat16)
        hidden32 = hidden.astype(jnp.float32)
        expert_out = jnp.einsum("escf,edf->escd", hidden32, down32).astype(jnp.bfloat16)
        flat_out = pad_row(expert_out.transpose(1, 0, 2, 3).reshape(expert_devs, EXPERTS * CAP, D), 1)
        picked = jnp.take_along_axis(flat_out, flat_positions, axis=1).reshape(expert_devs, TOK_DEV, TOPK, D)
        weights32 = block_weights.astype(jnp.float32)
        mixed = jnp.einsum("stk,stkd->std", weights32, picked.astype(jnp.float32)).astype(jnp.bfloat16)
        weight_slots = jnp.take_along_axis(pad_row(weights32.reshape(expert_devs, TOK_DEV * TOPK), 1), pair_tables, axis=1)
        grad_rows = jnp.take_along_axis(pad_row(block_upstream, 1), row_tables[..., None], axis=1)
        grad_out = (grad_rows.astype(jnp.float32) * weight_slots[..., None]).astype(jnp.bfloat16)
        grad_out = grad_out.reshape(expert_devs, EXPERTS, CAP, D).transpose(1, 0, 2, 3)
        grad_out32 = grad_out.astype(jnp.float32)
        grad_hidden = jnp.einsum("escd,edf->escf", grad_out32, down32)
        sigmoid_gate = jax.nn.sigmoid(gate_pre)
        grad_up_pre = (grad_hidden * gate_pre * sigmoid_gate).astype(jnp.bfloat16)
        grad_gate_pre = (grad_hidden * up_pre * sigmoid_gate * (1.0 + gate_pre * (1.0 - sigmoid_gate))).astype(jnp.bfloat16)
        gate_grad32 = grad_gate_pre.astype(jnp.float32)
        up_grad32 = grad_up_pre.astype(jnp.float32)
        grad_in = jnp.einsum("escf,edf->escd", gate_grad32, gate32) + jnp.einsum("escf,edf->escd", up_grad32, up32)
        grad_in = grad_in.astype(jnp.bfloat16)
        flat_grads = pad_row(grad_in.transpose(1, 0, 2, 3).reshape(expert_devs, EXPERTS * CAP, D), 1)
        grad_picked = jnp.take_along_axis(flat_grads, flat_positions, axis=1).reshape(expert_devs, TOK_DEV, TOPK, D)
        token_grads = jnp.sum(grad_picked.astype(jnp.float32), axis=2).astype(jnp.bfloat16)
        gate_part = jnp.einsum("escd,escf->edf", inputs32, gate_grad32)
        up_part = jnp.einsum("escd,escf->edf", inputs32, up_grad32)
        down_part = jnp.einsum("escd,escf->edf", grad_out32, hidden32)
        totals = (accumulate(totals[0], gate_part), accumulate(totals[1], up_part), accumulate(totals[2], down_part))
        return totals, (mixed, token_grads)

    zeros_grad = jnp.zeros((EXPERTS, D, FF), jnp.float32)
    totals, outputs = lax.scan(group, (zeros_grad, zeros_grad, zeros_grad), (token_blocks, id_blocks, slot_blocks, weight_blocks, upstream))
    mixed_all, grads_all = outputs
    inverse = jax.vmap(jax.vmap(invert_slots))(owner_slot)
    ordered = jnp.take_along_axis(mixed_all, inverse[..., None], axis=2)
    talker_out = ordered.reshape(data_devs, expert_devs, data_devs, PER_OWNER, D).transpose(2, 1, 0, 3, 4).reshape(TOKENS, D)
    grad_tokens = grads_all.reshape(TOKENS, D)
    factor = 1.0 / data_devs
    return talker_out, grad_tokens, totals[0] * factor, totals[1] * factor, totals[2] * factor
```

```python
import functools

import jax
import jax.numpy as jnp
from jax import lax
from jax.experimental import pallas as pl
from jax.experimental.pallas import tpu as pltpu
from jax.sharding import PartitionSpec as P

EXPERTS = 16
CAP = 64
MESH = pl.DeviceIdType.MESH
BF = jnp.bfloat16
F32 = jnp.float32
VMEM = pl.BlockSpec(memory_space=pltpu.VMEM)


def remote(src, dst, send, recv, where):
    return pltpu.make_async_remote_copy(
        src_ref=src, dst_ref=dst, send_sem=send, recv_sem=recv, device_id=where, device_id_type=MESH
    )


def greet(experts, data):
    c, s = lax.axis_index("expert"), lax.axis_index("dp")
    barrier = pltpu.get_barrier_semaphore()
    for k in range(1, experts):
        pl.semaphore_signal(
            barrier, inc=1, device_id={"expert": lax.rem(c + k, experts)}, device_id_type=MESH
        )
    for k in range(1, data):
        pl.semaphore_signal(
            barrier, inc=1, device_id={"dp": lax.rem(s + k, data)}, device_id_type=MESH
        )
    pl.semaphore_wait(barrier, experts + data - 2)


def gather_kernel(
    experts, data, tok, meta, gt, tok_all, meta_all, up_all, gs, gr, ts, tr, ms, mr, us, ur
):
    c, s = lax.axis_index("expert"), lax.axis_index("dp")
    greet(experts, data)
    grads, rows, metas, ups = [], [], [], []
    for k in range(1, data):
        peer = lax.rem(s + k, data)
        grads.append(
            remote(gt.at[peer], up_all.at[c, s], gs.at[k - 1], gr.at[k - 1], {"dp": peer})
        )
        grads[-1].start()
    for k in range(1, experts):
        peer = {"expert": lax.rem(c + k, experts)}
        metas.append(remote(meta, meta_all.at[c], ms.at[k - 1], mr.at[k - 1], peer))
        metas[-1].start()
        rows.append(remote(tok, tok_all.at[c], ts.at[k - 1], tr.at[k - 1], peer))
        rows[-1].start()
    tok_all[c] = tok[...]
    meta_all[c] = meta[...]
    up_all[c, s] = gt[s]
    for copy in grads:
        copy.wait_recv()
    for k in range(1, experts):
        peer = {"expert": lax.rem(c + k, experts)}
        ups.append(remote(up_all.at[c], up_all.at[c], us.at[k - 1], ur.at[k - 1], peer))
        ups[-1].start()
    for copy in grads:
        copy.wait_send()
    for copy in metas + rows + ups:
        copy.wait()


def gather_all(tokens, meta, owner_grads):
    experts, data = lax.axis_size("expert"), lax.axis_size("dp")
    dma = pltpu.SemaphoreType.DMA
    return pl.pallas_call(
        functools.partial(gather_kernel, experts, data),
        out_shape=(
            jax.ShapeDtypeStruct((experts,) + tokens.shape, BF),
            jax.ShapeDtypeStruct((experts,) + meta.shape, F32),
            jax.ShapeDtypeStruct((experts,) + owner_grads.shape, BF),
        ),
        in_specs=[VMEM] * 3,
        out_specs=(VMEM,) * 3,
        scratch_shapes=[dma((data - 1,))] * 2 + [dma((experts - 1,))] * 6,
        compiler_params=pltpu.CompilerParams(collective_id=0, has_side_effects=True),
    )(tokens, meta, owner_grads)


def dot(a, b, ca, cb):
    return lax.dot_general(a, b, (((ca,), (cb,)), ((), ())), preferred_element_type=F32)


def compute_kernel(
    local, tok, meta, up, gw, uw, dw, mixed, gtok, parts, dmat, cmat, xs, gs, outs, gins
):
    e = pl.program_id(0)
    blocks, rows, width = tok.shape
    slots = local * CAP
    pairs = meta.shape[1] // 3

    @pl.when(e == 0)
    def _():
        base = (lax.axis_index("expert") * slots).astype(F32)
        want = lax.broadcasted_iota(jnp.int32, (slots, rows), 0).astype(F32) + base
        for b in range(blocks):
            hit = jnp.zeros((slots, rows), F32)
            held = jnp.zeros((slots, rows), F32)
            for k in range(pairs):
                hit = jnp.where(meta[b, k : k + 1, :] == want, 1.0, hit)
                held = jnp.where(
                    meta[b, pairs + k : pairs + k + 1, :] == want,
                    meta[b, 2 * pairs + k : 2 * pairs + k + 1, :],
                    held,
                )
            dmat[b] = hit.astype(BF)
            cmat[b] = held.astype(BF)
            xs[b] = dot(dmat[b], tok[b], 1, 0).astype(BF)
            gs[b] = dot(cmat[b], up[b], 1, 0).astype(BF)

    here = pl.ds(pl.multiple_of(e * CAP, CAP), CAP)
    x = xs[:, here, :].reshape(blocks * CAP, width)
    g = gs[:, here, :].reshape(blocks * CAP, width)
    gate = dot(x, gw[0], 1, 0)
    upv = dot(x, uw[0], 1, 0)
    sig = 1.0 / (1.0 + jnp.exp(-gate))
    hidden = (gate * sig * upv).astype(BF)
    gh = dot(g, dw[0], 1, 0)
    gu = (gh * gate * sig).astype(BF)
    gg = (gh * upv * sig * (1.0 + gate * (1.0 - sig))).astype(BF)
    outs[:, here, :] = dot(hidden, dw[0], 1, 1).astype(BF).reshape(blocks, CAP, width)
    gin = dot(gg, gw[0], 1, 1) + dot(gu, uw[0], 1, 1)
    gins[:, here, :] = gin.astype(BF).reshape(blocks, CAP, width)
    parts[0, 0] = dot(x, gg, 0, 0).astype(BF)
    parts[1, 0] = dot(x, gu, 0, 0).astype(BF)
    parts[2, 0] = dot(g, hidden, 0, 0).astype(BF)

    @pl.when(e == local - 1)
    def _():
        for b in range(blocks):
            mixed[b] = dot(cmat[b], outs[b], 0, 0).astype(BF)
            gtok[b] = dot(dmat[b], gins[b], 0, 0).astype(BF)


def compute_all(tok, meta, up, gate_weight, up_weight, down_weight):
    local, width, ff = gate_weight.shape
    blocks, rows, _ = tok.shape
    slots = local * CAP
    whole = lambda shape: pl.BlockSpec(shape, lambda e: (0,) * len(shape))
    weight = pl.BlockSpec((1, width, ff), lambda e: (e, 0, 0))
    return pl.pallas_call(
        functools.partial(compute_kernel, local),
        grid=(local,),
        out_shape=(
            jax.ShapeDtypeStruct((blocks, rows, width), BF),
            jax.ShapeDtypeStruct((blocks, rows, width), BF),
            jax.ShapeDtypeStruct((3, local, width, ff), BF),
        ),
        in_specs=[whole(tok.shape), whole(meta.shape), whole(up.shape), weight, weight, weight],
        out_specs=(
            whole((blocks, rows, width)),
            whole((blocks, rows, width)),
            pl.BlockSpec((3, 1, width, ff), lambda e: (0, e, 0, 0)),
        ),
        scratch_shapes=[
            pltpu.VMEM((blocks, slots, rows), BF),
            pltpu.VMEM((blocks, slots, rows), BF),
            pltpu.VMEM((blocks, slots, width), BF),
            pltpu.VMEM((blocks, slots, width), BF),
            pltpu.VMEM((blocks, slots, width), BF),
            pltpu.VMEM((blocks, slots, width), BF),
        ],
        compiler_params=pltpu.CompilerParams(vmem_limit_bytes=56 * 2**20),
    )(tok, meta, up, gate_weight, up_weight, down_weight)


def reduce_kernel(
    experts, nz, nx, part, mixed, gtok, total, talk, grads,
    xrecv, xsum, below, above, mrecv, grecv, msum,
    xss, xrs, bss, brs, ass, ars, mss, mrs, gss, grs, tss, trs,
):
    data = nz * nx
    c, s = lax.axis_index("expert"), lax.axis_index("dp")
    z, x = lax.div(s, nx), lax.rem(s, nx)
    chunks = part.shape[0]
    greet(experts, data)

    def xcopy(i, k):
        px = lax.rem(x + k, nx)
        return remote(
            part.at[i, :, px], xrecv.at[k - 1, i], xss.at[k - 1, i], xrs.at[k - 1, i],
            {"dp": z * nx + px},
        )

    def upcopy(i, d):
        return remote(
            xsum.at[i, d], below.at[i, d], bss.at[i, d], brs.at[i, d], {"dp": lax.rem(s + nx, data)}
        )

    def downcopy(i, d):
        return remote(
            xsum.at[i, d], above.at[i, d], ass.at[i, d], ars.at[i, d],
            {"dp": lax.rem(s + data - nx, data)},
        )

    @pl.loop(0, chunks)
    def _(i):
        for k in range(1, nx):
            xcopy(i, k).start()

    backs, talks = [], []
    for k in range(1, experts):
        peer = lax.rem(c + k, experts)
        backs.append(
            remote(mixed.at[peer], mrecv.at[k - 1], mss.at[k - 1], mrs.at[k - 1], {"expert": peer})
        )
        backs[-1].start()
    grad_backs = []
    for k in range(1, experts):
        peer = lax.rem(c + k, experts)
        grad_backs.append(
            remote(gtok.at[peer], grecv.at[k - 1], gss.at[k - 1], grs.at[k - 1], {"expert": peer})
        )
        grad_backs[-1].start()

    def step(i):
        @pl.when(i < chunks)
        def _():
            for k in range(1, nx):
                xcopy(i, k).wait_recv()
            for d in range(nz):
                held = part[i, d, x].astype(F32)
                for k in range(1, nx):
                    held = held + xrecv[k - 1, i, d].astype(F32)
                xsum[i, d] = held.astype(BF)

        rise = i - z

        @pl.when((rise >= 0) & (rise < chunks))
        def _():
            for d in range(1, nz):
                @pl.when((z > 0) & (z < d))
                def _():
                    upcopy(rise, d).wait_recv()
                    xsum[rise, d] = (
                        xsum[rise, d].astype(F32) + below[rise, d].astype(F32)
                    ).astype(BF)

                @pl.when(z < d)
                def _():
                    upcopy(rise, d).start()

        fall = i - (nz - 1 - z)

        @pl.when((fall >= 0) & (fall < chunks))
        def _():
            for d in range(nz - 1):
                @pl.when((z < nz - 1) & (z > d))
                def _():
                    downcopy(fall, d).wait_recv()
                    xsum[fall, d] = (
                        xsum[fall, d].astype(F32) + above[fall, d].astype(F32)
                    ).astype(BF)

                @pl.when(z > d)
                def _():
                    downcopy(fall, d).start()

        last = i - (nz - 1)

        @pl.when(last >= 0)
        def _():
            total[last] = xsum[last, z].astype(F32) * (1.0 / data)

            @pl.when(z > 0)
            def _():
                upcopy(last, z).wait_recv()
                total[last] += below[last, z].astype(F32) * (1.0 / data)

            @pl.when(z < nz - 1)
            def _():
                downcopy(last, z).wait_recv()
                total[last] += above[last, z].astype(F32) * (1.0 / data)

    early = min(2, chunks)
    pl.loop(0, early)(step)

    for copy in backs:
        copy.wait_recv()
    held = mixed[c].astype(F32)
    for k in range(experts - 1):
        held = held + mrecv[k].astype(F32)
    msum[...] = held.astype(BF)
    for k in range(1, data):
        peer = lax.rem(s + k, data)
        talks.append(remote(msum.at[peer], talk.at[s], tss.at[k - 1], trs.at[k - 1], {"dp": peer}))
        talks[-1].start()
    talk[s] = msum[s]
    for copy in grad_backs:
        copy.wait_recv()
    held = gtok[c].astype(F32)
    for k in range(experts - 1):
        held = held + grecv[k].astype(F32)
    grads[...] = held.astype(BF)

    pl.loop(early, chunks + nz - 1)(step)

    for copy in backs + grad_backs:
        copy.wait_send()
    for copy in talks:
        copy.wait()

    @pl.loop(0, chunks)
    def _(i):
        for k in range(1, nx):
            xcopy(i, k).wait_send()
        for d in range(nz):
            @pl.when(d > z)
            def _():
                upcopy(i, d).wait_send()

            @pl.when(d < z)
            def _():
                downcopy(i, d).wait_send()


def reduce_all(parts, mixed, gtok):
    experts, data = lax.axis_size("expert"), lax.axis_size("dp")
    nx = 1 << ((data.bit_length() - 1) // 2)
    nz = data // nx
    three, local, width, ff = parts.shape
    chunks, rows = three * local, width // data
    blocks, tok_rows, _ = mixed.shape
    per_owner = tok_rows // data
    parts = parts.reshape(chunks, nz, nx, rows, ff)
    mixed = mixed.reshape(blocks, data, per_owner, width)
    dma = pltpu.SemaphoreType.DMA
    return pl.pallas_call(
        functools.partial(reduce_kernel, experts, nz, nx),
        out_shape=(
            jax.ShapeDtypeStruct((chunks, rows, ff), F32),
            jax.ShapeDtypeStruct((data, per_owner, width), BF),
            jax.ShapeDtypeStruct((tok_rows, width), BF),
        ),
        in_specs=[VMEM] * 3,
        out_specs=(VMEM,) * 3,
        scratch_shapes=[
            pltpu.VMEM((nx - 1, chunks, nz, rows, ff), BF),
            pltpu.VMEM((chunks, nz, rows, ff), BF),
            pltpu.VMEM((chunks, nz, rows, ff), BF),
            pltpu.VMEM((chunks, nz, rows, ff), BF),
            pltpu.VMEM((experts - 1, data, per_owner, width), BF),
            pltpu.VMEM((experts - 1, tok_rows, width), BF),
            pltpu.VMEM((data, per_owner, width), BF),
            dma((nx - 1, chunks)),
            dma((nx - 1, chunks)),
            dma((chunks, nz)),
            dma((chunks, nz)),
            dma((chunks, nz)),
            dma((chunks, nz)),
            dma((experts - 1,)),
            dma((experts - 1,)),
            dma((experts - 1,)),
            dma((experts - 1,)),
            dma((data - 1,)),
            dma((data - 1,)),
        ],
        compiler_params=pltpu.CompilerParams(
            collective_id=1, has_side_effects=True, vmem_limit_bytes=56 * 2**20
        ),
    )(parts, mixed, gtok)


def on_device(
    tokens,
    expert_ids,
    slot_index,
    combine_weight,
    talker_owner,
    gate_weight,
    up_weight,
    down_weight,
    grad_talker,
):
    data = lax.axis_size("dp")
    rows, width = tokens.shape
    per_owner = rows // data
    local = gate_weight.shape[0]
    order = jnp.arange(rows, dtype=jnp.int32)
    same = (talker_owner[:, None] == talker_owner[None, :]) & (order[:, None] < order[None, :])
    owner_slot = talker_owner * per_owner + jnp.sum(same.astype(jnp.int32), axis=0)
    position = jnp.where(slot_index >= 0, expert_ids * CAP + slot_index, -1).astype(F32).T
    weight = combine_weight.astype(F32).T
    pick = owner_slot[None, :] == order[:, None]
    moved = jnp.sum(
        jnp.where(pick[None], jnp.concatenate([position, weight], 0)[:, None, :], 0.0), axis=2
    )
    meta = jnp.concatenate([position, moved], 0)
    tok_all, meta_all, up_all = gather_all(
        tokens, meta, grad_talker.reshape(data, per_owner, width)
    )
    mixed, gtok, parts = compute_all(
        tok_all,
        meta_all,
        up_all.reshape(tok_all.shape),
        gate_weight,
        up_weight,
        down_weight,
    )
    total, talk, grad_tokens = reduce_all(parts, mixed, gtok)
    return (
        talk.reshape(rows, width),
        grad_tokens,
        total[:local],
        total[local : 2 * local],
        total[2 * local :],
    )


def solution(mesh):
    placed = (
        P(("dp", "expert"), None),
        P(("dp", "expert"), None),
        P(("dp", "expert"), None),
        P(("dp", "expert"), None),
        P(("dp", "expert")),
        P("expert", None, None),
        P("expert", None, None),
        P("expert", None, None),
        P(("dp", "expert"), None),
    )
    return jax.shard_map(
        on_device,
        mesh=mesh,
        in_specs=placed,
        out_specs=(
            P(("dp", "expert"), None),
            P(("dp", "expert"), None),
            P("expert", "dp", None),
            P("expert", "dp", None),
            P("expert", "dp", None),
        ),
        check_vma=False,
    )
```

```python
import functools

import jax
import jax.numpy as jnp
from jax import lax
from jax.experimental import pallas as pl
from jax.experimental.pallas import tpu as pltpu
from jax.sharding import PartitionSpec as P

EXPERTS = 16
CAP = 64
MESH = pl.DeviceIdType.MESH
BF = jnp.bfloat16
F32 = jnp.float32
VMEM = pl.BlockSpec(memory_space=pltpu.VMEM)


def remote(src, dst, send, recv, where):
    return pltpu.make_async_remote_copy(
        src_ref=src, dst_ref=dst, send_sem=send, recv_sem=recv, device_id=where, device_id_type=MESH
    )


def greet(experts, data):
    c, s = lax.axis_index("expert"), lax.axis_index("dp")
    barrier = pltpu.get_barrier_semaphore()
    for k in range(1, experts):
        pl.semaphore_signal(
            barrier, inc=1, device_id={"expert": lax.rem(c + k, experts)}, device_id_type=MESH
        )
    for k in range(1, data):
        pl.semaphore_signal(
            barrier, inc=1, device_id={"dp": lax.rem(s + k, data)}, device_id_type=MESH
        )
    pl.semaphore_wait(barrier, experts + data - 2)


def dot(a, b, ca, cb):
    return lax.dot_general(a, b, (((ca,), (cb,)), ((), ())), preferred_element_type=F32)


def layer_kernel(
    experts, nz, nx, tok, meta, gt, gate_hbm, up_hbm, down_hbm,
    out_gate, out_up, out_down, talk, grads,
    tok_all, meta_all, up_all, gw, uw, dw, dmat, cmat, xs, gs, outs, gins, gates, ups, hid,
    mixed, gtok, part, xrecv, line, mrecv, grecv, msum, acc,
    wsem, gs_s, gr_s, ts_s, tr_s, fs_s, fr_s, ms_s, mr_s, us_s, ur_s, vs_s, vr_s,
    xs_s, xr_s, bs_s, br_s, as_s, ar_s, bks, bkr, gks, gkr, tks, tkr,
):
    data = nz * nx
    c, s = lax.axis_index("expert"), lax.axis_index("dp")
    z, x = lax.div(s, nx), lax.rem(s, nx)
    sibling = c + 1 - 2 * lax.rem(c, 2)
    half = experts // 2
    local, width, ff = gw.shape
    blocks, rows, _ = tok_all.shape
    slots = local * CAP
    pairs = meta.shape[0] // 3
    chunks = 3 * local

    loads = [
        pltpu.make_async_copy(gate_hbm, gw, wsem.at[0]),
        pltpu.make_async_copy(up_hbm, uw, wsem.at[1]),
        pltpu.make_async_copy(down_hbm, dw, wsem.at[2]),
    ]
    for copy in loads:
        copy.start()
    greet(experts, data)

    def shared(src, buf, send, recv):
        copies = []
        for k in range(1, half):
            peer = lax.rem(c + 2 * k, experts)
            copies.append(remote(src, buf.at[c], send.at[k], recv.at[k], {"expert": peer}))
        copies.append(remote(src, buf.at[c], send.at[0], recv.at[0], {"expert": sibling}))
        for copy in copies:
            copy.start()
        return copies

    def passed(copies, buf, send, recv):
        handed = []
        for k in range(1, half):
            copies[k - 1].wait_recv()
            came = lax.rem(c + experts - 2 * k, experts)
            handed.append(
                remote(
                    buf.at[came], buf.at[came], send.at[k - 1], recv.at[k - 1], {"expert": sibling}
                )
            )
            handed[-1].start()
        return handed

    def arrived(copies, handed):
        copies[-1].wait_recv()
        for copy in handed:
            copy.wait_recv()

    owner_grads, metas = [], []
    for k in range(1, data):
        peer = lax.rem(s + k, data)
        owner_grads.append(
            remote(gt.at[peer], up_all.at[c, s], gs_s.at[k - 1], gr_s.at[k - 1], {"dp": peer})
        )
        owner_grads[-1].start()
    for k in range(1, experts):
        peer = {"expert": lax.rem(c + k, experts)}
        metas.append(remote(meta, meta_all.at[c], ms_s.at[k - 1], mr_s.at[k - 1], peer))
        metas[-1].start()
    tok_sent = shared(tok, tok_all, ts_s, tr_s)
    tok_all[c] = tok[...]
    meta_all[c] = meta[...]
    up_all[c, s] = gt[s]
    for copy in owner_grads:
        copy.wait_recv()
    up_sent = shared(up_all.at[c], up_all, us_s, ur_s)
    tok_passed = passed(tok_sent, tok_all, fs_s, fr_s)

    for copy in metas:
        copy.wait_recv()
    base = (c * slots).astype(F32)
    want = lax.broadcasted_iota(jnp.int32, (slots, rows), 0).astype(F32) + base

    @pl.loop(0, blocks)
    def _(b):
        hit = jnp.zeros((slots, rows), F32)
        held = jnp.zeros((slots, rows), F32)
        for k in range(pairs):
            hit = jnp.where(meta_all[b, k : k + 1, :] == want, 1.0, hit)
            held = jnp.where(
                meta_all[b, pairs + k : pairs + k + 1, :] == want,
                meta_all[b, 2 * pairs + k : 2 * pairs + k + 1, :],
                held,
            )
        dmat[b] = hit.astype(BF)
        cmat[b] = held.astype(BF)

    arrived(tok_sent, tok_passed)

    @pl.loop(0, blocks)
    def _(b):
        xs[b] = dot(dmat[b], tok_all[b], 1, 0).astype(BF)

    up_passed = passed(up_sent, up_all, vs_s, vr_s)
    for copy in loads:
        copy.wait()

    def slot_rows(e):
        return pl.ds(pl.multiple_of(e * CAP, CAP), CAP)

    @pl.loop(0, local)
    def _(e):
        rows_x = xs[:, slot_rows(e), :].reshape(blocks * CAP, width)
        gate = dot(rows_x, gw[e], 1, 0)
        upv = dot(rows_x, uw[e], 1, 0)
        hidden = (gate * (1.0 / (1.0 + jnp.exp(-gate))) * upv).astype(BF)
        gates[e] = gate
        ups[e] = upv
        hid[e] = hidden

    arrived(up_sent, up_passed)

    @pl.loop(0, blocks)
    def _(b):
        gs[b] = dot(cmat[b], up_all[b].reshape(rows, width), 1, 0).astype(BF)

    def xcopy(i, k):
        px = lax.rem(x + k, nx)
        return remote(
            part.at[i, :, px], xrecv.at[k - 1, i], xs_s.at[k - 1, i], xr_s.at[k - 1, i],
            {"dp": z * nx + px},
        )

    def upcopy(i, d):
        return remote(
            xrecv.at[0, i, d], line.at[i, d + 1], bs_s.at[i, d], br_s.at[i, d],
            {"dp": lax.rem(s + nx, data)},
        )

    def downcopy(i, d):
        return remote(
            xrecv.at[0, i, d], line.at[i, d], as_s.at[i, d], ar_s.at[i, d],
            {"dp": lax.rem(s + data - nx, data)},
        )

    def emit(i, left, right):
        part[i] = dot(left, right, 0, 0).astype(BF).reshape(part.shape[1:])
        for k in range(1, nx):
            xcopy(i, k).start()

    @pl.loop(0, local)
    def _(e):
        rows_x = xs[:, slot_rows(e), :].reshape(blocks * CAP, width)
        rows_g = gs[:, slot_rows(e), :].reshape(blocks * CAP, width)
        emit(3 * e, rows_g, hid[e])
        gate, upv = gates[e], ups[e]
        sig = 1.0 / (1.0 + jnp.exp(-gate))
        gh = dot(rows_g, dw[e], 1, 0)
        gu = (gh * gate * sig).astype(BF)
        gg = (gh * upv * sig * (1.0 + gate * (1.0 - sig))).astype(BF)
        emit(3 * e + 1, rows_x, gg)
        emit(3 * e + 2, rows_x, gu)
        gin = dot(gg, gw[e], 1, 1) + dot(gu, uw[e], 1, 1)
        gins[:, slot_rows(e), :] = gin.astype(BF).reshape(blocks, CAP, width)
        outs[:, slot_rows(e), :] = dot(hid[e], dw[e], 1, 1).astype(BF).reshape(blocks, CAP, width)

    @pl.loop(0, blocks)
    def _(b):
        mixed[b] = dot(cmat[b], outs[b], 0, 0).astype(BF).reshape(mixed.shape[1:])
        gtok[b] = dot(dmat[b], gins[b], 0, 0).astype(BF)

    backs, grad_backs, talks = [], [], []
    for k in range(1, experts):
        peer = lax.rem(c + k, experts)
        backs.append(
            remote(mixed.at[peer], mrecv.at[k - 1], bks.at[k - 1], bkr.at[k - 1], {"expert": peer})
        )
        backs[-1].start()
    for k in range(1, experts):
        peer = lax.rem(c + k, experts)
        grad_backs.append(
            remote(gtok.at[peer], grecv.at[k - 1], gks.at[k - 1], gkr.at[k - 1], {"expert": peer})
        )
        grad_backs[-1].start()

    def step(i):
        @pl.when(i < chunks)
        def _():
            for k in range(1, nx):
                xcopy(i, k).wait_recv()
            for d in range(nz):
                held = part[i, d, x].astype(F32)
                for k in range(1, nx):
                    held = held + xrecv[k - 1, i, d].astype(F32)
                xrecv[0, i, d] = held.astype(BF)

        rise = i - z

        @pl.when((rise >= 0) & (rise < chunks))
        def _():
            for d in range(1, nz):
                @pl.when((z > 0) & (z < d))
                def _():
                    upcopy(rise, d).wait_recv()
                    xrecv[0, rise, d] = (
                        xrecv[0, rise, d].astype(F32) + line[rise, d + 1].astype(F32)
                    ).astype(BF)

                @pl.when(z < d)
                def _():
                    upcopy(rise, d).start()

        fall = i - (nz - 1 - z)

        @pl.when((fall >= 0) & (fall < chunks))
        def _():
            for d in range(nz - 1):
                @pl.when((z < nz - 1) & (z > d))
                def _():
                    downcopy(fall, d).wait_recv()
                    xrecv[0, fall, d] = (
                        xrecv[0, fall, d].astype(F32) + line[fall, d].astype(F32)
                    ).astype(BF)

                @pl.when(z > d)
                def _():
                    downcopy(fall, d).start()

        last = i - (nz - 1)

        @pl.when(last >= 0)
        def _():
            acc[...] = xrecv[0, last, z].astype(F32)

            @pl.when(z > 0)
            def _():
                upcopy(last, z).wait_recv()
                acc[...] += line[last, z + 1].astype(F32)

            @pl.when(z < nz - 1)
            def _():
                downcopy(last, z).wait_recv()
                acc[...] += line[last, z].astype(F32)

            e = lax.div(last, 3)
            for m, out in enumerate((out_down, out_gate, out_up)):
                @pl.when(lax.rem(last, 3) == m)
                def _():
                    out[e] = acc[...] * (1.0 / data)

    early = min(3, chunks)
    pl.loop(0, early)(step)

    for copy in backs:
        copy.wait_recv()
    held = mixed[c].astype(F32)
    for k in range(experts - 1):
        held = held + mrecv[k].astype(F32)
    msum[...] = held.astype(BF)
    for k in range(1, data):
        peer = lax.rem(s + k, data)
        talks.append(remote(msum.at[peer], talk.at[s], tks.at[k - 1], tkr.at[k - 1], {"dp": peer}))
        talks[-1].start()
    talk[s] = msum[s]
    for copy in grad_backs:
        copy.wait_recv()
    held = gtok[c].astype(F32)
    for k in range(experts - 1):
        held = held + grecv[k].astype(F32)
    grads[...] = held.astype(BF)

    pl.loop(early, chunks + nz - 1)(step)

    for copy in owner_grads + metas + tok_sent + tok_passed + up_sent + up_passed:
        copy.wait_send()
    for copy in backs + grad_backs:
        copy.wait_send()
    for copy in talks:
        copy.wait()

    @pl.loop(0, chunks)
    def _(i):
        for k in range(1, nx):
            xcopy(i, k).wait_send()
        for d in range(nz):
            @pl.when(d > z)
            def _():
                upcopy(i, d).wait_send()

            @pl.when(d < z)
            def _():
                downcopy(i, d).wait_send()


def layer(tokens, meta, owner_grads, gate_weight, up_weight, down_weight):
    experts, data = lax.axis_size("expert"), lax.axis_size("dp")
    nx = 1 << ((data.bit_length() - 1) // 2)
    nz = data // nx
    local, width, ff = gate_weight.shape
    rows, _ = tokens.shape
    per_owner = rows // data
    chunks, piece = 3 * local, width // data
    slots = local * CAP
    half = experts // 2
    grad_shape = jax.ShapeDtypeStruct((local, piece, ff), F32)
    dma = pltpu.SemaphoreType.DMA
    mem = pltpu.VMEM
    hbm = pl.BlockSpec(memory_space=pl.ANY)
    two = lambda *shape: [dma(shape), dma(shape)]
    return pl.pallas_call(
        functools.partial(layer_kernel, experts, nz, nx),
        out_shape=(
            grad_shape,
            grad_shape,
            grad_shape,
            jax.ShapeDtypeStruct((data, per_owner, width), BF),
            jax.ShapeDtypeStruct((rows, width), BF),
        ),
        in_specs=[VMEM] * 3 + [hbm] * 3,
        out_specs=(VMEM,) * 5,
        scratch_shapes=[
            mem((experts, rows, width), BF),
            mem((experts,) + meta.shape, F32),
            mem((experts, data, per_owner, width), BF),
            mem((local, width, ff), BF),
            mem((local, width, ff), BF),
            mem((local, width, ff), BF),
            mem((experts, slots, rows), BF),
            mem((experts, slots, rows), BF),
            mem((experts, slots, width), BF),
            mem((experts, slots, width), BF),
            mem((experts, slots, width), BF),
            mem((experts, slots, width), BF),
            mem((local, experts * CAP, ff), F32),
            mem((local, experts * CAP, ff), F32),
            mem((local, experts * CAP, ff), BF),
            mem((experts, data, per_owner, width), BF),
            mem((experts, rows, width), BF),
            mem((chunks, nz, nx, piece, ff), BF),
            mem((nx - 1, chunks, nz, piece, ff), BF),
            mem((chunks, nz + 1, piece, ff), BF),
            mem((experts - 1, data, per_owner, width), BF),
            mem((experts - 1, rows, width), BF),
            mem((data, per_owner, width), BF),
            mem((piece, ff), F32),
            dma((3,)),
        ]
        + two(data - 1)
        + two(half)
        + two(half)
        + two(experts - 1)
        + two(half)
        + two(half)
        + two(nx - 1, chunks)
        + two(chunks, nz)
        + two(chunks, nz)
        + two(experts - 1)
        + two(experts - 1)
        + two(data - 1),
        compiler_params=pltpu.CompilerParams(
            collective_id=0, has_side_effects=True, vmem_limit_bytes=62 * 2**20
        ),
    )(tokens, meta, owner_grads, gate_weight, up_weight, down_weight)


def on_device(
    tokens,
    expert_ids,
    slot_index,
    combine_weight,
    talker_owner,
    gate_weight,
    up_weight,
    down_weight,
    grad_talker,
):
    data = lax.axis_size("dp")
    rows, width = tokens.shape
    per_owner = rows // data
    order = jnp.arange(rows, dtype=jnp.int32)
    same = (talker_owner[:, None] == talker_owner[None, :]) & (order[:, None] < order[None, :])
    owner_slot = talker_owner * per_owner + jnp.sum(same.astype(jnp.int32), axis=0)
    position = jnp.where(slot_index >= 0, expert_ids * CAP + slot_index, -1).astype(F32).T
    weight = combine_weight.astype(F32).T
    pick = owner_slot[None, :] == order[:, None]
    moved = jnp.sum(
        jnp.where(pick[None], jnp.concatenate([position, weight], 0)[:, None, :], 0.0), axis=2
    )
    meta = jnp.concatenate([position, moved], 0)
    grad_gate, grad_up, grad_down, talk, grad_tokens = layer(
        tokens,
        meta,
        grad_talker.reshape(data, per_owner, width),
        gate_weight,
        up_weight,
        down_weight,
    )
    return (talk.reshape(rows, width), grad_tokens, grad_gate, grad_up, grad_down)


def solution(mesh):
    placed = (
        P(("dp", "expert"), None),
        P(("dp", "expert"), None),
        P(("dp", "expert"), None),
        P(("dp", "expert"), None),
        P(("dp", "expert")),
        P("expert", None, None),
        P("expert", None, None),
        P("expert", None, None),
        P(("dp", "expert"), None),
    )
    return jax.shard_map(
        on_device,
        mesh=mesh,
        in_specs=placed,
        out_specs=(
            P(("dp", "expert"), None),
            P(("dp", "expert"), None),
            P("expert", "dp", None),
            P("expert", "dp", None),
            P("expert", "dp", None),
        ),
        check_vma=False,
    )
```

```python
import functools

import jax
import jax.numpy as jnp
from jax import lax
from jax.experimental import pallas as pl
from jax.experimental.pallas import tpu as pltpu
from jax.sharding import PartitionSpec as P

EXPERTS = 16
CAP = 64
MESH = pl.DeviceIdType.MESH
BF = jnp.bfloat16
F32 = jnp.float32
VMEM = pl.BlockSpec(memory_space=pltpu.VMEM)


def remote(src, dst, send, recv, where):
    return pltpu.make_async_remote_copy(
        src_ref=src, dst_ref=dst, send_sem=send, recv_sem=recv, device_id=where, device_id_type=MESH
    )


def greet(experts, data):
    c, s = lax.axis_index("expert"), lax.axis_index("dp")
    barrier = pltpu.get_barrier_semaphore()
    for k in range(1, experts):
        pl.semaphore_signal(
            barrier, inc=1, device_id={"expert": lax.rem(c + k, experts)}, device_id_type=MESH
        )
    for k in range(1, data):
        pl.semaphore_signal(
            barrier, inc=1, device_id={"dp": lax.rem(s + k, data)}, device_id_type=MESH
        )
    pl.semaphore_wait(barrier, experts + data - 2)


def dot(a, b, ca, cb):
    return lax.dot_general(a, b, (((ca,), (cb,)), ((), ())), preferred_element_type=F32)


def layer_kernel(
    experts, nz, nx, tok, meta, gt, gate_hbm, up_hbm, down_hbm,
    total, talk, grads,
    tok_all, meta_all, up_all, gw, uw, dw, dmat, cmat, xs, gs, outs, gins, gates, ups, hid,
    mixed, gtok, part, xrecv, line, zline, xlast, mrecv, grecv, msum, acc,
    wsem, gs_s, gr_s, ts_s, tr_s, fs_s, fr_s, ms_s, mr_s, us_s, ur_s, vs_s, vr_s,
    xs_s, xr_s, bs_s, br_s, as_s, ar_s, zb_s, zb_r, za_s, za_r, xl_s, xl_r, bks, bkr, gks, gkr, tks, tkr,
):
    data = nz * nx
    c, s = lax.axis_index("expert"), lax.axis_index("dp")
    z, x = lax.div(s, nx), lax.rem(s, nx)
    sibling = c + 1 - 2 * lax.rem(c, 2)
    half = experts // 2
    local, width, ff = gw.shape
    blocks, rows, _ = tok_all.shape
    slots = local * CAP
    pairs = meta.shape[0] // 4
    chunks = 3 * local
    first = chunks // 6

    loads = [
        pltpu.make_async_copy(gate_hbm, gw, wsem.at[0]),
        pltpu.make_async_copy(up_hbm, uw, wsem.at[1]),
        pltpu.make_async_copy(down_hbm, dw, wsem.at[2]),
    ]
    for copy in loads:
        copy.start()
    greet(experts, data)

    def shared(src, buf, send, recv):
        copies = []
        for k in range(1, half):
            peer = lax.rem(c + 2 * k, experts)
            copies.append(remote(src, buf.at[c], send.at[k], recv.at[k], {"expert": peer}))
        copies.append(remote(src, buf.at[c], send.at[0], recv.at[0], {"expert": sibling}))
        for copy in copies:
            copy.start()
        return copies

    def passed(copies, buf, send, recv):
        handed = []
        for k in range(1, half):
            copies[k - 1].wait_recv()
            came = lax.rem(c + experts - 2 * k, experts)
            handed.append(
                remote(
                    buf.at[came], buf.at[came], send.at[k - 1], recv.at[k - 1], {"expert": sibling}
                )
            )
            handed[-1].start()
        return handed

    def arrived(copies, handed):
        copies[-1].wait_recv()
        for copy in handed:
            copy.wait_recv()

    owner_grads, metas = [], []
    for k in range(1, data):
        peer = lax.rem(s + k, data)
        owner_grads.append(
            remote(gt.at[peer], up_all.at[c, s], gs_s.at[k - 1], gr_s.at[k - 1], {"dp": peer})
        )
        owner_grads[-1].start()
    for k in range(1, experts):
        peer = {"expert": lax.rem(c + k, experts)}
        metas.append(remote(meta, meta_all.at[c], ms_s.at[k - 1], mr_s.at[k - 1], peer))
        metas[-1].start()
    tok_sent = shared(tok, tok_all, ts_s, tr_s)
    tok_all[c] = tok[...]
    meta_all[c] = meta[...]
    up_all[c, s] = gt[s]
    for copy in owner_grads:
        copy.wait_recv()
    up_sent = shared(up_all.at[c], up_all, us_s, ur_s)
    tok_passed = passed(tok_sent, tok_all, fs_s, fr_s)

    for copy in metas:
        copy.wait_recv()
    base = (c * slots).astype(F32)
    want = lax.broadcasted_iota(jnp.int32, (slots, rows), 0).astype(F32) + base

    wide = max(16, data)
    kinds = lax.broadcasted_iota(jnp.int32, (wide, rows), 0).astype(F32)
    line_of = lax.broadcasted_iota(jnp.int32, (rows, rows), 0)
    earlier = (line_of < lax.broadcasted_iota(jnp.int32, (rows, rows), 1)).astype(F32).astype(BF)
    line_of = line_of.astype(F32)

    @pl.loop(0, blocks)
    def _(b):
        slot = meta_all[b, pairs : 2 * pairs, :]
        place = jnp.where(slot >= 0.0, meta_all[b, 0:pairs, :] * CAP + slot, -1.0)
        weight = meta_all[b, 2 * pairs : 3 * pairs, :]
        hit = jnp.zeros((slots, rows), F32)
        held = jnp.zeros((slots, rows), F32)
        for k in range(pairs):
            here = place[k : k + 1, :] == want
            hit = jnp.where(here, 1.0, hit)
            held = jnp.where(here, weight[k : k + 1, :], held)
        dmat[b] = hit.astype(BF)
        owner = meta_all[b, 3 * pairs : 3 * pairs + 1, :]
        owned = (kinds == owner).astype(F32)
        before = dot(owned.astype(BF), earlier, 1, 0)
        owner_slot = owner * (rows // data) + jnp.sum(owned * before, axis=0, keepdims=True)
        pick = (line_of == owner_slot).astype(F32).astype(BF)
        cmat[b] = dot(held.astype(BF), pick, 1, 1).astype(BF)

    arrived(tok_sent, tok_passed)

    @pl.loop(0, blocks)
    def _(b):
        xs[b] = dot(dmat[b], tok_all[b], 1, 0).astype(BF)

    up_passed = passed(up_sent, up_all, vs_s, vr_s)
    for copy in loads:
        copy.wait()

    def slot_rows(e):
        return pl.ds(pl.multiple_of(e * CAP, CAP), CAP)

    @pl.loop(0, local)
    def _(e):
        rows_x = xs[:, slot_rows(e), :].reshape(blocks * CAP, width)
        gate = dot(rows_x, gw[e], 1, 0)
        upv = dot(rows_x, uw[e], 1, 0)
        hidden = (gate * (1.0 / (1.0 + jnp.exp(-gate))) * upv).astype(BF)
        gates[e] = gate
        ups[e] = upv
        hid[e] = hidden

    arrived(up_sent, up_passed)

    @pl.loop(0, blocks)
    def _(b):
        gs[b] = dot(cmat[b], up_all[b].reshape(rows, width), 1, 0).astype(BF)

    def xcopy(i, k):
        px = lax.rem(x + k, nx)
        return remote(
            part.at[i, :, px], xrecv.at[k - 1, i], xs_s.at[k - 1, i], xr_s.at[k - 1, i],
            {"dp": z * nx + px},
        )

    def upcopy(i, d):
        return remote(
            xrecv.at[0, i, d], line.at[i, d + 1], bs_s.at[i, d], br_s.at[i, d],
            {"dp": lax.rem(s + nx, data)},
        )

    def downcopy(i, d):
        return remote(
            xrecv.at[0, i, d], line.at[i, d], as_s.at[i, d], ar_s.at[i, d],
            {"dp": lax.rem(s + data - nx, data)},
        )

    def zup(i, d):
        return remote(
            part.at[i, d], zline.at[i, d + 1], zb_s.at[i, d], zb_r.at[i, d],
            {"dp": lax.rem(s + nx, data)},
        )

    def zdown(i, d):
        return remote(
            part.at[i, d], zline.at[i, d], za_s.at[i, d], za_r.at[i, d],
            {"dp": lax.rem(s + data - nx, data)},
        )

    def zlast(i, k):
        px = lax.rem(x + k, nx)
        return remote(
            part.at[i, z, px], xlast.at[k - 1, i], xl_s.at[k - 1, i], xl_r.at[k - 1, i],
            {"dp": z * nx + px},
        )

    def emit(i, left, right):
        part[i] = dot(left, right, 0, 0).astype(BF).reshape(part.shape[1:])

        @pl.when(i >= first)
        def _():
            for k in range(1, nx):
                xcopy(i, k).start()

        if first:
            for d in range(nz):
                if d > 0:
                    @pl.when((i < first) & (z == 0))
                    def _():
                        zup(i, d).start()

                if d < nz - 1:
                    @pl.when((i < first) & (z == nz - 1))
                    def _():
                        zdown(i, d).start()

    def zstep(i):
        rise = i - z

        @pl.when((z > 0) & (rise >= 0) & (rise < first))
        def _():
            for d in range(1, nz):
                @pl.when(z < d)
                def _():
                    zup(rise, d).wait_recv()
                    part[rise, d] = (
                        part[rise, d].astype(F32) + zline[rise, d + 1].astype(F32)
                    ).astype(BF)
                    zup(rise, d).start()

        fall = i - (nz - 1 - z)

        @pl.when((z < nz - 1) & (fall >= 0) & (fall < first))
        def _():
            for d in range(nz - 1):
                @pl.when(z > d)
                def _():
                    zdown(fall, d).wait_recv()
                    part[fall, d] = (
                        part[fall, d].astype(F32) + zline[fall, d].astype(F32)
                    ).astype(BF)
                    zdown(fall, d).start()

        last = i - (nz - 1)

        @pl.when((last >= 0) & (last < first))
        def _():
            @pl.when(z > 0)
            def _():
                zup(last, z).wait_recv()
                part[last, z] = (
                    part[last, z].astype(F32) + zline[last, z + 1].astype(F32)
                ).astype(BF)

            @pl.when(z < nz - 1)
            def _():
                zdown(last, z).wait_recv()
                part[last, z] = (
                    part[last, z].astype(F32) + zline[last, z].astype(F32)
                ).astype(BF)

            for k in range(1, nx):
                zlast(last, k).start()

    @pl.loop(0, local)
    def _(e):
        rows_x = xs[:, slot_rows(e), :].reshape(blocks * CAP, width)
        rows_g = gs[:, slot_rows(e), :].reshape(blocks * CAP, width)
        emit(3 * e, rows_g, hid[e])
        gate, upv = gates[e], ups[e]
        sig = 1.0 / (1.0 + jnp.exp(-gate))
        gh = dot(rows_g, dw[e], 1, 0)
        gu = (gh * gate * sig).astype(BF)
        gg = (gh * upv * sig * (1.0 + gate * (1.0 - sig))).astype(BF)
        emit(3 * e + 1, rows_x, gg)
        emit(3 * e + 2, rows_x, gu)
        gin = dot(gg, gw[e], 1, 1) + dot(gu, uw[e], 1, 1)
        gins[:, slot_rows(e), :] = gin.astype(BF).reshape(blocks, CAP, width)
        outs[:, slot_rows(e), :] = dot(hid[e], dw[e], 1, 1).astype(BF).reshape(blocks, CAP, width)

    @pl.loop(0, blocks)
    def _(b):
        mixed[b] = dot(cmat[b], outs[b], 0, 0).astype(BF).reshape(mixed.shape[1:])
        gtok[b] = dot(dmat[b], gins[b], 0, 0).astype(BF)

    backs, grad_backs, talks = [], [], []
    for k in range(1, experts):
        peer = lax.rem(c + k, experts)
        backs.append(
            remote(mixed.at[peer], mrecv.at[k - 1], bks.at[k - 1], bkr.at[k - 1], {"expert": peer})
        )
        backs[-1].start()
    for k in range(1, experts):
        peer = lax.rem(c + k, experts)
        grad_backs.append(
            remote(gtok.at[peer], grecv.at[k - 1], gks.at[k - 1], gkr.at[k - 1], {"expert": peer})
        )
        grad_backs[-1].start()

    def step(i):
        if first:
            zstep(i)

        @pl.when((i >= first) & (i < chunks))
        def _():
            for k in range(1, nx):
                xcopy(i, k).wait_recv()
            for d in range(nz):
                held = part[i, d, x].astype(F32)
                for k in range(1, nx):
                    held = held + xrecv[k - 1, i, d].astype(F32)
                xrecv[0, i, d] = held.astype(BF)

        rise = i - z

        @pl.when((rise >= first) & (rise < chunks))
        def _():
            for d in range(1, nz):
                @pl.when((z > 0) & (z < d))
                def _():
                    upcopy(rise, d).wait_recv()
                    xrecv[0, rise, d] = (
                        xrecv[0, rise, d].astype(F32) + line[rise, d + 1].astype(F32)
                    ).astype(BF)

                @pl.when(z < d)
                def _():
                    upcopy(rise, d).start()

        fall = i - (nz - 1 - z)

        @pl.when((fall >= first) & (fall < chunks))
        def _():
            for d in range(nz - 1):
                @pl.when((z < nz - 1) & (z > d))
                def _():
                    downcopy(fall, d).wait_recv()
                    xrecv[0, fall, d] = (
                        xrecv[0, fall, d].astype(F32) + line[fall, d].astype(F32)
                    ).astype(BF)

                @pl.when(z > d)
                def _():
                    downcopy(fall, d).start()

        last = i - (nz - 1)

        @pl.when(last >= first)
        def _():
            acc[...] = xrecv[0, last, z].astype(F32)

            @pl.when(z > 0)
            def _():
                upcopy(last, z).wait_recv()
                acc[...] += line[last, z + 1].astype(F32)

            @pl.when(z < nz - 1)
            def _():
                downcopy(last, z).wait_recv()
                acc[...] += line[last, z].astype(F32)

            total[lax.rem(last, 3) * local + lax.div(last, 3)] = acc[...] * (1.0 / data)

    early = min(first + 3, chunks)
    late = chunks - 1
    pl.loop(0, early)(step)

    for copy in backs:
        copy.wait_recv()
    held = mixed[c].astype(F32)
    for k in range(experts - 1):
        held = held + mrecv[k].astype(F32)
    msum[...] = held.astype(BF)
    for k in range(1, data):
        peer = lax.rem(s + k, data)
        talks.append(remote(msum.at[peer], talk.at[s], tks.at[k - 1], tkr.at[k - 1], {"dp": peer}))
        talks[-1].start()
    talk[s] = msum[s]
    for copy in grad_backs:
        copy.wait_recv()
    held = gtok[c].astype(F32)
    for k in range(experts - 1):
        held = held + grecv[k].astype(F32)
    grads[...] = held.astype(BF)

    pl.loop(early, late)(step)

    for i in range(first):
        held = part[i, z, x].astype(F32)
        for k in range(1, nx):
            zlast(i, k).wait_recv()
            held = held + xlast[k - 1, i].astype(F32)
        total[i % 3 * local + i // 3] = held * (1.0 / data)

    pl.loop(max(early, late), chunks + nz - 1)(step)

    for copy in owner_grads + metas + tok_sent + tok_passed + up_sent + up_passed:
        copy.wait_send()
    for copy in backs + grad_backs:
        copy.wait_send()
    for copy in talks:
        copy.wait()

    @pl.loop(first, chunks)
    def _(i):
        for k in range(1, nx):
            xcopy(i, k).wait_send()
        for d in range(nz):
            @pl.when(d > z)
            def _():
                upcopy(i, d).wait_send()

            @pl.when(d < z)
            def _():
                downcopy(i, d).wait_send()

    for i in range(first):
        for k in range(1, nx):
            zlast(i, k).wait_send()
        for d in range(nz):
            @pl.when(d > z)
            def _():
                zup(i, d).wait_send()

            @pl.when(d < z)
            def _():
                zdown(i, d).wait_send()


def layer(tokens, meta, owner_grads, gate_weight, up_weight, down_weight):
    experts, data = lax.axis_size("expert"), lax.axis_size("dp")
    nx = 1 << ((data.bit_length() - 1) // 2)
    nz = data // nx
    local, width, ff = gate_weight.shape
    rows, _ = tokens.shape
    per_owner = rows // data
    chunks, piece = 3 * local, width // data
    lead = max(1, chunks // 6)
    slots = local * CAP
    half = experts // 2
    dma = pltpu.SemaphoreType.DMA
    mem = pltpu.VMEM
    hbm = pl.BlockSpec(memory_space=pl.ANY)
    two = lambda *shape: [dma(shape), dma(shape)]
    return pl.pallas_call(
        functools.partial(layer_kernel, experts, nz, nx),
        out_shape=(
            jax.ShapeDtypeStruct((chunks, piece, ff), F32),
            jax.ShapeDtypeStruct((data, per_owner, width), BF),
            jax.ShapeDtypeStruct((rows, width), BF),
        ),
        in_specs=[VMEM] * 3 + [hbm] * 3,
        out_specs=(VMEM,) * 3,
        scratch_shapes=[
            mem((experts, rows, width), BF),
            mem((experts,) + meta.shape, F32),
            mem((experts, data, per_owner, width), BF),
            mem((local, width, ff), BF),
            mem((local, width, ff), BF),
            mem((local, width, ff), BF),
            mem((experts, slots, rows), BF),
            mem((experts, slots, rows), BF),
            mem((experts, slots, width), BF),
            mem((experts, slots, width), BF),
            mem((experts, slots, width), BF),
            mem((experts, slots, width), BF),
            mem((local, experts * CAP, ff), F32),
            mem((local, experts * CAP, ff), F32),
            mem((local, experts * CAP, ff), BF),
            mem((experts, data, per_owner, width), BF),
            mem((experts, rows, width), BF),
            mem((chunks, nz, nx, piece, ff), BF),
            mem((nx - 1, chunks, nz, piece, ff), BF),
            mem((chunks, nz + 1, piece, ff), BF),
            mem((lead, nz + 1, nx, piece, ff), BF),
            mem((nx - 1, lead, piece, ff), BF),
            mem((experts - 1, data, per_owner, width), BF),
            mem((experts - 1, rows, width), BF),
            mem((data, per_owner, width), BF),
            mem((piece, ff), F32),
            dma((3,)),
        ]
        + two(data - 1)
        + two(half)
        + two(half)
        + two(experts - 1)
        + two(half)
        + two(half)
        + two(nx - 1, chunks)
        + two(chunks, nz)
        + two(chunks, nz)
        + two(lead, nz)
        + two(lead, nz)
        + two(nx - 1, lead)
        + two(experts - 1)
        + two(experts - 1)
        + two(data - 1),
        compiler_params=pltpu.CompilerParams(
            collective_id=0, has_side_effects=True, vmem_limit_bytes=62 * 2**20
        ),
    )(tokens, meta, owner_grads, gate_weight, up_weight, down_weight)


def on_device(
    tokens,
    expert_ids,
    slot_index,
    combine_weight,
    talker_owner,
    gate_weight,
    up_weight,
    down_weight,
    grad_talker,
):
    data = lax.axis_size("dp")
    rows, width = tokens.shape
    per_owner = rows // data
    pairs = expert_ids.shape[1]
    meta = jnp.concatenate(
        [
            expert_ids.astype(F32),
            slot_index.astype(F32),
            combine_weight.astype(F32),
            jnp.broadcast_to(talker_owner.astype(F32)[:, None], (rows, pairs)),
        ],
        1,
    ).T
    total, talk, grad_tokens = layer(
        tokens,
        meta,
        grad_talker.reshape(data, per_owner, width),
        gate_weight,
        up_weight,
        down_weight,
    )
    local = gate_weight.shape[0]
    return (
        talk.reshape(rows, width),
        grad_tokens,
        total[local : 2 * local],
        total[2 * local :],
        total[:local],
    )


def solution(mesh):
    placed = (
        P(("dp", "expert"), None),
        P(("dp", "expert"), None),
        P(("dp", "expert"), None),
        P(("dp", "expert"), None),
        P(("dp", "expert")),
        P("expert", None, None),
        P("expert", None, None),
        P("expert", None, None),
        P(("dp", "expert"), None),
    )
    return jax.shard_map(
        on_device,
        mesh=mesh,
        in_specs=placed,
        out_specs=(
            P(("dp", "expert"), None),
            P(("dp", "expert"), None),
            P("expert", "dp", None),
            P("expert", "dp", None),
            P("expert", "dp", None),
        ),
        check_vma=False,
    )
```

```python
import functools

import jax
import jax.numpy as jnp
from jax import lax
from jax.experimental import pallas as pl
from jax.experimental.pallas import tpu as pltpu
from jax.sharding import PartitionSpec as P

EXPERTS = 16
CAP = 64
MESH = pl.DeviceIdType.MESH
BF = jnp.bfloat16
F32 = jnp.float32
VMEM = pl.BlockSpec(memory_space=pltpu.VMEM)


def remote(src, dst, send, recv, where):
    return pltpu.make_async_remote_copy(
        src_ref=src, dst_ref=dst, send_sem=send, recv_sem=recv, device_id=where, device_id_type=MESH
    )


def greet(experts, data):
    c, s = lax.axis_index("expert"), lax.axis_index("dp")
    barrier = pltpu.get_barrier_semaphore()
    for k in range(1, experts):
        pl.semaphore_signal(
            barrier, inc=1, device_id={"expert": lax.rem(c + k, experts)}, device_id_type=MESH
        )
    for k in range(1, data):
        pl.semaphore_signal(
            barrier, inc=1, device_id={"dp": lax.rem(s + k, data)}, device_id_type=MESH
        )
    pl.semaphore_wait(barrier, experts + data - 2)


def dot(a, b, ca, cb):
    return lax.dot_general(a, b, (((ca,), (cb,)), ((), ())), preferred_element_type=F32)


def layer_kernel(
    experts, nz, nx, tok, ids, slot_ids, shares, owners, gt, gate_hbm, up_hbm, down_hbm,
    total, talk, grads,
    meta, tok_all, meta_all, up_all, gw, uw, dw, dmat, cmat, xs, gs, outs, gins, gates, ups, hid,
    mixed, gtok, part, xrecv, line, zline, xlast, mrecv, grecv, msum, acc,
    wsem, gs_s, gr_s, ts_s, tr_s, fs_s, fr_s, ms_s, mr_s, us_s, ur_s, vs_s, vr_s,
    xs_s, xr_s, bs_s, br_s, as_s, ar_s, zb_s, zb_r, za_s, za_r, xl_s, xl_r, bks, bkr, gks, gkr, tks, tkr,
):
    data = nz * nx
    c, s = lax.axis_index("expert"), lax.axis_index("dp")
    z, x = lax.div(s, nx), lax.rem(s, nx)
    sibling = c + 1 - 2 * lax.rem(c, 2)
    half = experts // 2
    local, width, ff = gw.shape
    blocks, rows, _ = tok_all.shape
    slots = local * CAP
    pairs = meta.shape[0] // 4
    chunks = 3 * local
    first = chunks // 6

    loads = [
        pltpu.make_async_copy(gate_hbm, gw, wsem.at[0]),
        pltpu.make_async_copy(up_hbm, uw, wsem.at[1]),
        pltpu.make_async_copy(down_hbm, dw, wsem.at[2]),
    ]
    for copy in loads:
        copy.start()
    greet(experts, data)

    def shared(src, buf, send, recv):
        copies = []
        for k in range(1, half):
            peer = lax.rem(c + 2 * k, experts)
            copies.append(remote(src, buf.at[c], send.at[k], recv.at[k], {"expert": peer}))
        copies.append(remote(src, buf.at[c], send.at[0], recv.at[0], {"expert": sibling}))
        for copy in copies:
            copy.start()
        return copies

    def passed(copies, buf, send, recv):
        handed = []
        for k in range(1, half):
            copies[k - 1].wait_recv()
            came = lax.rem(c + experts - 2 * k, experts)
            handed.append(
                remote(
                    buf.at[came], buf.at[came], send.at[k - 1], recv.at[k - 1], {"expert": sibling}
                )
            )
            handed[-1].start()
        return handed

    def arrived(copies, handed):
        copies[-1].wait_recv()
        for copy in handed:
            copy.wait_recv()

    owner_grads, metas = [], []
    for k in range(1, data):
        peer = lax.rem(s + k, data)
        owner_grads.append(
            remote(gt.at[peer], up_all.at[c, s], gs_s.at[k - 1], gr_s.at[k - 1], {"dp": peer})
        )
        owner_grads[-1].start()
    tok_sent = shared(tok, tok_all, ts_s, tr_s)
    line_of = lax.broadcasted_iota(jnp.int32, (rows, rows), 0)
    across = lax.broadcasted_iota(jnp.int32, (rows, rows), 1)
    for k, table in enumerate((ids, slot_ids, shares)):
        meta[k * pairs : (k + 1) * pairs, :] = table[...].astype(F32)
    meta[3 * pairs :, :] = jnp.broadcast_to(owners[...].astype(F32), (pairs, rows))
    for k in range(1, experts):
        peer = {"expert": lax.rem(c + k, experts)}
        metas.append(remote(meta, meta_all.at[c], ms_s.at[k - 1], mr_s.at[k - 1], peer))
        metas[-1].start()
    tok_all[c] = tok[...]
    meta_all[c] = meta[...]
    up_all[c, s] = gt[s]
    for copy in owner_grads:
        copy.wait_recv()
    up_sent = shared(up_all.at[c], up_all, us_s, ur_s)
    tok_passed = passed(tok_sent, tok_all, fs_s, fr_s)

    for copy in metas:
        copy.wait_recv()
    base = (c * slots).astype(F32)
    want = lax.broadcasted_iota(jnp.int32, (slots, rows), 0).astype(F32) + base

    wide = max(16, data)
    kinds = lax.broadcasted_iota(jnp.int32, (wide, rows), 0).astype(F32)
    earlier = (line_of < across).astype(F32).astype(BF)
    line_of = line_of.astype(F32)

    @pl.loop(0, blocks)
    def _(b):
        slot = meta_all[b, pairs : 2 * pairs, :]
        place = jnp.where(slot >= 0.0, meta_all[b, 0:pairs, :] * CAP + slot, -1.0)
        weight = meta_all[b, 2 * pairs : 3 * pairs, :]
        hit = jnp.zeros((slots, rows), F32)
        held = jnp.zeros((slots, rows), F32)
        for k in range(pairs):
            here = place[k : k + 1, :] == want
            hit = jnp.where(here, 1.0, hit)
            held = jnp.where(here, weight[k : k + 1, :], held)
        dmat[b] = hit.astype(BF)
        owner = meta_all[b, 3 * pairs : 3 * pairs + 1, :]
        owned = (kinds == owner).astype(F32)
        before = dot(owned.astype(BF), earlier, 1, 0)
        owner_slot = owner * (rows // data) + jnp.sum(owned * before, axis=0, keepdims=True)
        pick = (line_of == owner_slot).astype(F32).astype(BF)
        cmat[b] = dot(held.astype(BF), pick, 1, 1).astype(BF)

    arrived(tok_sent, tok_passed)

    @pl.loop(0, blocks)
    def _(b):
        xs[b] = dot(dmat[b], tok_all[b], 1, 0).astype(BF)

    for copy in loads:
        copy.wait()

    def slot_rows(e):
        return pl.ds(pl.multiple_of(e * CAP, CAP), CAP)

    @pl.loop(0, local)
    def _(e):
        rows_x = xs[:, slot_rows(e), :].reshape(blocks * CAP, width)
        gate = dot(rows_x, gw[e], 1, 0)
        upv = dot(rows_x, uw[e], 1, 0)
        hidden = (gate * (1.0 / (1.0 + jnp.exp(-gate))) * upv).astype(BF)
        gates[e] = gate
        ups[e] = upv
        hid[e] = hidden

    up_passed = passed(up_sent, up_all, vs_s, vr_s)
    arrived(up_sent, up_passed)

    @pl.loop(0, blocks)
    def _(b):
        gs[b] = dot(cmat[b], up_all[b].reshape(rows, width), 1, 0).astype(BF)

    def xcopy(i, k):
        px = lax.rem(x + k, nx)
        return remote(
            part.at[i, :, px], xrecv.at[k - 1, i], xs_s.at[k - 1, i], xr_s.at[k - 1, i],
            {"dp": z * nx + px},
        )

    def upcopy(i, d):
        return remote(
            xrecv.at[0, i, d], line.at[i, d + 1], bs_s.at[i, d], br_s.at[i, d],
            {"dp": lax.rem(s + nx, data)},
        )

    def downcopy(i, d):
        return remote(
            xrecv.at[0, i, d], line.at[i, d], as_s.at[i, d], ar_s.at[i, d],
            {"dp": lax.rem(s + data - nx, data)},
        )

    def zup(i, d):
        return remote(
            part.at[i, d], zline.at[i, d + 1], zb_s.at[i, d], zb_r.at[i, d],
            {"dp": lax.rem(s + nx, data)},
        )

    def zdown(i, d):
        return remote(
            part.at[i, d], zline.at[i, d], za_s.at[i, d], za_r.at[i, d],
            {"dp": lax.rem(s + data - nx, data)},
        )

    def zlast(i, k):
        px = lax.rem(x + k, nx)
        return remote(
            part.at[i, z, px], xlast.at[k - 1, i], xl_s.at[k - 1, i], xl_r.at[k - 1, i],
            {"dp": z * nx + px},
        )

    def emit(i, left, right):
        part[i] = dot(left, right, 0, 0).astype(BF).reshape(part.shape[1:])

        @pl.when(i >= first)
        def _():
            for k in range(1, nx):
                xcopy(i, k).start()

        if first:
            for d in range(nz):
                if d > 0:
                    @pl.when((i < first) & (z == 0))
                    def _():
                        zup(i, d).start()

                if d < nz - 1:
                    @pl.when((i < first) & (z == nz - 1))
                    def _():
                        zdown(i, d).start()

    def zstep(i):
        rise = i - z

        @pl.when((z > 0) & (rise >= 0) & (rise < first))
        def _():
            for d in range(1, nz):
                @pl.when(z < d)
                def _():
                    zup(rise, d).wait_recv()
                    part[rise, d] = (
                        part[rise, d].astype(F32) + zline[rise, d + 1].astype(F32)
                    ).astype(BF)
                    zup(rise, d).start()

        fall = i - (nz - 1 - z)

        @pl.when((z < nz - 1) & (fall >= 0) & (fall < first))
        def _():
            for d in range(nz - 1):
                @pl.when(z > d)
                def _():
                    zdown(fall, d).wait_recv()
                    part[fall, d] = (
                        part[fall, d].astype(F32) + zline[fall, d].astype(F32)
                    ).astype(BF)
                    zdown(fall, d).start()

        last = i - (nz - 1)

        @pl.when((last >= 0) & (last < first))
        def _():
            @pl.when(z > 0)
            def _():
                zup(last, z).wait_recv()
                part[last, z] = (
                    part[last, z].astype(F32) + zline[last, z + 1].astype(F32)
                ).astype(BF)

            @pl.when(z < nz - 1)
            def _():
                zdown(last, z).wait_recv()
                part[last, z] = (
                    part[last, z].astype(F32) + zline[last, z].astype(F32)
                ).astype(BF)

            for k in range(1, nx):
                zlast(last, k).start()

    @pl.loop(0, local)
    def _(e):
        rows_x = xs[:, slot_rows(e), :].reshape(blocks * CAP, width)
        rows_g = gs[:, slot_rows(e), :].reshape(blocks * CAP, width)
        emit(3 * e, rows_g, hid[e])
        gate, upv = gates[e], ups[e]
        sig = 1.0 / (1.0 + jnp.exp(-gate))
        gh = dot(rows_g, dw[e], 1, 0)
        gu = (gh * gate * sig).astype(BF)
        gg = (gh * upv * sig * (1.0 + gate * (1.0 - sig))).astype(BF)
        emit(3 * e + 1, rows_x, gg)
        emit(3 * e + 2, rows_x, gu)
        gin = dot(gg, gw[e], 1, 1) + dot(gu, uw[e], 1, 1)
        gins[:, slot_rows(e), :] = gin.astype(BF).reshape(blocks, CAP, width)
        outs[:, slot_rows(e), :] = dot(hid[e], dw[e], 1, 1).astype(BF).reshape(blocks, CAP, width)

    @pl.loop(0, blocks)
    def _(b):
        mixed[b] = dot(cmat[b], outs[b], 0, 0).astype(BF).reshape(mixed.shape[1:])
        gtok[b] = dot(dmat[b], gins[b], 0, 0).astype(BF)

    backs, grad_backs, talks = [], [], []
    for k in range(1, experts):
        peer = lax.rem(c + k, experts)
        backs.append(
            remote(mixed.at[peer], mrecv.at[k - 1], bks.at[k - 1], bkr.at[k - 1], {"expert": peer})
        )
        backs[-1].start()
    for k in range(1, experts):
        peer = lax.rem(c + k, experts)
        grad_backs.append(
            remote(gtok.at[peer], grecv.at[k - 1], gks.at[k - 1], gkr.at[k - 1], {"expert": peer})
        )
        grad_backs[-1].start()

    def step(i):
        if first:
            zstep(i)

        @pl.when((i >= first) & (i < chunks))
        def _():
            for k in range(1, nx):
                xcopy(i, k).wait_recv()
            for d in range(nz):
                held = part[i, d, x].astype(F32)
                for k in range(1, nx):
                    held = held + xrecv[k - 1, i, d].astype(F32)
                xrecv[0, i, d] = held.astype(BF)

        rise = i - z

        @pl.when((rise >= first) & (rise < chunks))
        def _():
            for d in range(1, nz):
                @pl.when((z > 0) & (z < d))
                def _():
                    upcopy(rise, d).wait_recv()
                    xrecv[0, rise, d] = (
                        xrecv[0, rise, d].astype(F32) + line[rise, d + 1].astype(F32)
                    ).astype(BF)

                @pl.when(z < d)
                def _():
                    upcopy(rise, d).start()

        fall = i - (nz - 1 - z)

        @pl.when((fall >= first) & (fall < chunks))
        def _():
            for d in range(nz - 1):
                @pl.when((z < nz - 1) & (z > d))
                def _():
                    downcopy(fall, d).wait_recv()
                    xrecv[0, fall, d] = (
                        xrecv[0, fall, d].astype(F32) + line[fall, d].astype(F32)
                    ).astype(BF)

                @pl.when(z > d)
                def _():
                    downcopy(fall, d).start()

        last = i - (nz - 1)

        @pl.when(last >= first)
        def _():
            acc[...] = xrecv[0, last, z].astype(F32)

            @pl.when(z > 0)
            def _():
                upcopy(last, z).wait_recv()
                acc[...] += line[last, z + 1].astype(F32)

            @pl.when(z < nz - 1)
            def _():
                downcopy(last, z).wait_recv()
                acc[...] += line[last, z].astype(F32)

            total[lax.rem(last, 3) * local + lax.div(last, 3)] = acc[...] * (1.0 / data)

    early = min(first + 3, chunks)
    late = chunks - 1
    pl.loop(0, early)(step)

    for copy in backs:
        copy.wait_recv()
    held = mixed[c].astype(F32)
    for k in range(experts - 1):
        held = held + mrecv[k].astype(F32)
    msum[...] = held.astype(BF)
    for k in range(1, data):
        peer = lax.rem(s + k, data)
        talks.append(remote(msum.at[peer], talk.at[s], tks.at[k - 1], tkr.at[k - 1], {"dp": peer}))
        talks[-1].start()
    talk[s] = msum[s]
    for copy in grad_backs:
        copy.wait_recv()
    held = gtok[c].astype(F32)
    for k in range(experts - 1):
        held = held + grecv[k].astype(F32)
    grads[...] = held.astype(BF)

    pl.loop(early, late)(step)

    for i in range(first):
        held = part[i, z, x].astype(F32)
        for k in range(1, nx):
            zlast(i, k).wait_recv()
            held = held + xlast[k - 1, i].astype(F32)
        total[i % 3 * local + i // 3] = held * (1.0 / data)

    pl.loop(max(early, late), chunks + nz - 1)(step)

    for copy in owner_grads + metas + tok_sent + tok_passed + up_sent + up_passed:
        copy.wait_send()
    for copy in backs + grad_backs:
        copy.wait_send()
    for copy in talks:
        copy.wait()

    @pl.loop(first, chunks)
    def _(i):
        for k in range(1, nx):
            xcopy(i, k).wait_send()
        for d in range(nz):
            @pl.when(d > z)
            def _():
                upcopy(i, d).wait_send()

            @pl.when(d < z)
            def _():
                downcopy(i, d).wait_send()

    for i in range(first):
        for k in range(1, nx):
            zlast(i, k).wait_send()
        for d in range(nz):
            @pl.when(d > z)
            def _():
                zup(i, d).wait_send()

            @pl.when(d < z)
            def _():
                zdown(i, d).wait_send()


def layer(
    tokens, ids, slot_ids, shares, owners, owner_grads, gate_weight, up_weight, down_weight
):
    experts, data = lax.axis_size("expert"), lax.axis_size("dp")
    nx = 1 << ((data.bit_length() - 1) // 2)
    nz = data // nx
    local, width, ff = gate_weight.shape
    rows, _ = tokens.shape
    per_owner = rows // data
    pairs = ids.shape[0]
    chunks, piece = 3 * local, width // data
    lead = max(1, chunks // 6)
    slots = local * CAP
    half = experts // 2
    dma = pltpu.SemaphoreType.DMA
    mem = pltpu.VMEM
    hbm = pl.BlockSpec(memory_space=pl.ANY)
    two = lambda *shape: [dma(shape), dma(shape)]
    return pl.pallas_call(
        functools.partial(layer_kernel, experts, nz, nx),
        out_shape=(
            jax.ShapeDtypeStruct((chunks, piece, ff), F32),
            jax.ShapeDtypeStruct((data, per_owner, width), BF),
            jax.ShapeDtypeStruct((rows, width), BF),
        ),
        in_specs=[VMEM] * 6 + [hbm] * 3,
        out_specs=(VMEM,) * 3,
        scratch_shapes=[
            mem((4 * pairs, rows), F32),
            mem((experts, rows, width), BF),
            mem((experts, 4 * pairs, rows), F32),
            mem((experts, data, per_owner, width), BF),
            mem((local, width, ff), BF),
            mem((local, width, ff), BF),
            mem((local, width, ff), BF),
            mem((experts, slots, rows), BF),
            mem((experts, slots, rows), BF),
            mem((experts, slots, width), BF),
            mem((experts, slots, width), BF),
            mem((experts, slots, width), BF),
            mem((experts, slots, width), BF),
            mem((local, experts * CAP, ff), F32),
            mem((local, experts * CAP, ff), F32),
            mem((local, experts * CAP, ff), BF),
            mem((experts, data, per_owner, width), BF),
            mem((experts, rows, width), BF),
            mem((chunks, nz, nx, piece, ff), BF),
            mem((nx - 1, chunks, nz, piece, ff), BF),
            mem((chunks, nz + 1, piece, ff), BF),
            mem((lead, nz + 1, nx, piece, ff), BF),
            mem((nx - 1, lead, piece, ff), BF),
            mem((experts - 1, data, per_owner, width), BF),
            mem((experts - 1, rows, width), BF),
            mem((data, per_owner, width), BF),
            mem((piece, ff), F32),
            dma((3,)),
        ]
        + two(data - 1)
        + two(half)
        + two(half)
        + two(experts - 1)
        + two(half)
        + two(half)
        + two(nx - 1, chunks)
        + two(chunks, nz)
        + two(chunks, nz)
        + two(lead, nz)
        + two(lead, nz)
        + two(nx - 1, lead)
        + two(experts - 1)
        + two(experts - 1)
        + two(data - 1),
        compiler_params=pltpu.CompilerParams(
            collective_id=0, has_side_effects=True, vmem_limit_bytes=62 * 2**20
        ),
    )(tokens, ids, slot_ids, shares, owners, owner_grads, gate_weight, up_weight, down_weight)


def on_device(
    tokens,
    expert_ids,
    slot_index,
    combine_weight,
    talker_owner,
    gate_weight,
    up_weight,
    down_weight,
    grad_talker,
):
    data = lax.axis_size("dp")
    rows, width = tokens.shape
    per_owner = rows // data
    total, talk, grad_tokens = layer(
        tokens,
        expert_ids.T,
        slot_index.T,
        combine_weight.T,
        talker_owner.reshape(1, rows),
        grad_talker.reshape(data, per_owner, width),
        gate_weight,
        up_weight,
        down_weight,
    )
    local = gate_weight.shape[0]
    return (
        talk.reshape(rows, width),
        grad_tokens,
        total[local : 2 * local],
        total[2 * local :],
        total[:local],
    )


def solution(mesh):
    placed = (
        P(("dp", "expert"), None),
        P(("dp", "expert"), None),
        P(("dp", "expert"), None),
        P(("dp", "expert"), None),
        P(("dp", "expert")),
        P("expert", None, None),
        P("expert", None, None),
        P("expert", None, None),
        P(("dp", "expert"), None),
    )
    return jax.shard_map(
        on_device,
        mesh=mesh,
        in_specs=placed,
        out_specs=(
            P(("dp", "expert"), None),
            P(("dp", "expert"), None),
            P("expert", "dp", None),
            P("expert", "dp", None),
            P("expert", "dp", None),
        ),
        check_vma=False,
    )
```
